128 devices in a mesh: az: 16 (over z, x_hi, core), dep: 8 (over y, x_lo).
Axes of the slice: x: 4 (x_hi: 2, x_lo: 2; x = x_hi * 2 + x_lo), y: 4, z: 4, core: 2. Of those that a mesh axis runs over, the one named last changes fastest.
Arguments:
- adjoint_in: float32 [2, 2048, 4096], P(None, 'az', 'dep'), may hold values from -6 to 6
- forward_field: float32 [8, 2, 2048, 4096], P(None, None, 'az', 'dep'), may hold values from -6 to 6
- screen: float32 [2048, 4096], P('az', 'dep'), may hold values from -3.140625 to 3.140625
- bed_weight: float32 [4096], replicated, may hold values from 0.1 to 1
- labels: int32 [2048, 32], P('az'), may hold values from 0 to 31
Outputs:
- adjoint_out: float32 [2, 2048, 4096], P(None, 'az', 'dep')
- sensitivity: float32 [32], replicated
The draws below stay inside these ranges and needn't reach their ends.
All inputs are finite; a program needn't handle non-finite values.
Results may differ from the reference program's by a relative error of at most 0.0003.
Values sent between devices are 32-bit elements; how exact they have to be, the bound alone decides.
No kernel may reach another device: no remote copies, remote signals or barrier semaphores. Data moves between devices by JAX's collectives and lax.ppermute only.
A program may use at most 128 MiB of HBM per device.

```python
import math
import jax
import jax.numpy as jnp

DEPTHS = 4096
AZIM = 2048
STEPS = 8
GROUPS = 32


def set_ends(entries, rng, smallest, largest):
    spot = [jax.random.randint(jax.random.fold_in(rng, axis), (), 0, length) for axis, length in enumerate(entries.shape)]
    longest = entries.shape.index(max(entries.shape))
    next_to = spot[:longest] + [(spot[longest] + 1) % entries.shape[longest]] + spot[longest + 1:]
    return entries.at[tuple(spot)].set(smallest).at[tuple(next_to)].set(largest)


def block_levels(own_key, extent, split, least, largest):
    factor_of = 1.0
    for position, shards_of in split:
        steps = jax.random.uniform(jax.random.fold_in(jax.random.fold_in(own_key, 6), position), (shards_of,), jnp.float32, least / len(split), largest / len(split))
        factor_of = factor_of * jnp.repeat(jnp.exp(steps), extent[position] // shards_of).reshape((-1,) + (1,) * (len(extent) - 1 - position))
    return factor_of


def scatter_about(key, dims, spread, most, cuts=(), kind=jnp.bfloat16):
    drawn = jax.random.normal(key, dims, jnp.float32) * spread
    if len(cuts) > 0:
        drawn = block_levels(key, dims, cuts, -0.22, 0.18) * drawn
    return jnp.clip(drawn, min=-most, max=most).astype(kind)


def setup_inputs(seed: int = 0) -> dict:
    seeds = jax.random.split(jax.random.key(seed), 6)
    adjoint_in = scatter_about(seeds[0], (2, AZIM, DEPTHS), 1.0, 6.0, ((1, 16), (2, 8)), jnp.float32)
    forward_field = scatter_about(seeds[1], (STEPS, 2, AZIM, DEPTHS), 1.0, 6.0, ((2, 16), (3, 8)), jnp.float32)
    screen = jnp.clip(jax.random.uniform(seeds[2], (AZIM, DEPTHS), jnp.float32, -3.140625, 3.140625), -3.140625, 3.140625)
    bed_weight = jnp.clip(jnp.exp(jax.random.uniform(seeds[3], (DEPTHS,), jnp.float32, math.log(0.1), math.log(1.0))), 0.1, 1.0)
    labels = set_ends(jax.random.randint(seeds[4], (AZIM, DEPTHS // 128), 0, GROUPS), jax.random.fold_in(seeds[4], 1), 0, GROUPS - 1).astype(jnp.int32)
    return dict(adjoint_in=adjoint_in, forward_field=forward_field, screen=screen, bed_weight=bed_weight, labels=labels)


def laplace(field):
    return jnp.roll(field, 1, 0) + jnp.roll(field, -1, 0) - 2.0 * field


def reference(adjoint_in, forward_field, screen, bed_weight, labels):
    coupling = 0.15
    mu = adjoint_in[0] + 1j * adjoint_in[1]
    freq = jnp.arange(DEPTHS)
    freq = jnp.where(freq < DEPTHS // 2, freq, freq - DEPTHS).astype(jnp.float32)
    beta = 30.0 * (freq / (DEPTHS // 2)) ** 2
    phase = jnp.cos(beta) + 1j * jnp.sin(beta)
    rotate = jnp.cos(screen) - 1j * jnp.sin(screen)
    sensitivity = jnp.zeros((GROUPS,), jnp.float32)
    for step in range(STEPS - 1, -1, -1):
        stored = forward_field[step]
        term = (jnp.imag(mu) * stored[0] - jnp.real(mu) * stored[1]) * bed_weight[None, :]
        blocks = term.reshape(AZIM, DEPTHS // 128, 128).sum(-1)
        sensitivity = sensitivity + jax.ops.segment_sum(blocks.reshape(-1), labels.reshape(-1), GROUPS)
        mu = mu * rotate
        lap = laplace(mu)
        mu = mu - 1j * coupling * lap - 0.5 * coupling * coupling * laplace(lap)
        mu = jnp.fft.ifft(jnp.fft.fft(mu, axis=1) * phase[None, :], axis=1)
    return jnp.stack([jnp.real(mu), jnp.imag(mu)]), sensitivity
```

```python
import math

import jax
import jax.numpy as jnp
import ml_dtypes
import numpy as np
from jax import lax
from jax.experimental import pallas as pl
from jax.experimental.pallas import tpu as pltpu
from jax.sharding import PartitionSpec as P

GROUPS = 32
COUPLING = 0.15
LABEL_BLOCK = 128
LANES = 128
ROW_PAD = 8


def split_table(table):
    high = table.astype(ml_dtypes.bfloat16)
    low = (table - high.astype(np.float64)).astype(ml_dtypes.bfloat16)
    return np.stack([high, low])


def transform_tables(depths):
    blocks = depths // LANES
    lane = np.arange(LANES)
    turn = 2.0 * np.pi * (np.outer(lane, lane) % LANES) / LANES
    cosine, sine = np.cos(turn), np.sin(turn)
    ahead = np.block([[cosine, -sine], [sine, cosine]])
    back = np.block([[cosine, sine], [-sine, cosine]])
    outer = np.arange(blocks)
    twist = 2.0 * np.pi * np.outer(outer, lane) / depths
    freq = outer[:, None] + blocks * lane[None, :]
    freq = np.where(freq < depths // 2, freq, freq - depths)
    beta = 30.0 * (freq / (depths // 2)) ** 2
    tables = np.stack([np.cos(twist), -np.sin(twist), np.cos(beta) / depths, np.sin(beta) / depths])
    return (
        split_table(ahead),
        split_table(back),
        tables[:, :, None, :].astype(np.float32),
    )


def times(value, factor):
    return (value[0] * factor[0] - value[1] * factor[1], value[0] * factor[1] + value[1] * factor[0])


def times_fixed(value, angle):
    c, s = math.cos(angle), math.sin(angle)
    if abs(s) < 1e-12:
        return value if c > 0 else (-value[0], -value[1])
    if abs(c) < 1e-12:
        return (-value[1], value[0]) if s > 0 else (value[1], -value[0])
    if abs(abs(c) - abs(s)) < 1e-12:
        root = math.sqrt(0.5)
        re = value[0] * math.copysign(1, c) - value[1] * math.copysign(1, s)
        im = value[0] * math.copysign(1, s) + value[1] * math.copysign(1, c)
        return (re * root, im * root)
    return (value[0] * c - value[1] * s, value[0] * s + value[1] * c)


def plus(a, b):
    return (a[0] + b[0], a[1] + b[1])


def minus(a, b):
    return (a[0] - b[0], a[1] - b[1])


def small_dft(values, sign):
    count = len(values)
    if count == 1:
        return values
    even = small_dft(values[0::2], sign)
    odd = small_dft(values[1::2], sign)
    odd = [times_fixed(v, sign * 2.0 * math.pi * k / count) for k, v in enumerate(odd)]
    return [plus(e, o) for e, o in zip(even, odd)] + [minus(e, o) for e, o in zip(even, odd)]


def sine_cosine(angle):
    half = 0.5 * angle
    square = half * half
    s = jnp.full_like(square, 1.0 / math.factorial(13))
    for order in (11, 9, 7, 5, 3, 1):
        s = s * square + (-1.0) ** (order // 2) / math.factorial(order)
    s = s * half
    c = jnp.full_like(square, 1.0 / math.factorial(12))
    for order in (10, 8, 6, 4, 2, 0):
        c = c * square + (-1.0) ** (order // 2) / math.factorial(order)
    return 2.0 * s * c, 1.0 - 2.0 * s * s


def steps_kernel(steps, halo, window, ahead, back, tables, past, out, scr, angle_c, angle_s, mid, high, low):
    outer, inner = mid.shape[1], mid.shape[2]
    blocks = outer * inner
    rows = window.shape[2]
    own = rows - 2 * halo
    root_angle = 2.0 * math.pi / blocks
    half = 0.5 * COUPLING * COUPLING

    scr[:, :, :, 0:ROW_PAD] = jnp.zeros((2, outer, inner, ROW_PAD, LANES), jnp.float32)
    scr[:, :, :, ROW_PAD + rows :] = jnp.zeros((2, outer, inner, ROW_PAD, LANES), jnp.float32)

    def turn_screen(value, p, q, base):
        c = angle_c[p, q, base : base + 8]
        s = angle_s[p, q, base : base + 8]
        scr[0, p, q, base + ROW_PAD : base + ROW_PAD + 8] = value[0] * c + value[1] * s
        scr[1, p, q, base + ROW_PAD : base + ROW_PAD + 8] = value[1] * c - value[0] * s

    def start(p, carry):
        for q in range(inner):
            lanes = slice(q * LANES, (q + 1) * LANES)
            for base in range(0, rows, 8):
                at = slice(base, base + 8)
                s, c = sine_cosine(window[p, 2, at, lanes])
                angle_c[p, q, at] = c
                angle_s[p, q, at] = s
                turn_screen((window[p, 0, at, lanes], window[p, 1, at, lanes]), p, q, base)
        return carry

    lax.fori_loop(0, outer, start, 0)

    def couple(p, q, base):
        def at(part, shift):
            begin = base + ROW_PAD + shift
            return scr[part, p, q, begin : begin + 8]

        centre = [at(part, 0) for part in range(2)]
        near = [at(part, 1) + at(part, -1) for part in range(2)]
        far = [at(part, 2) + at(part, -2) for part in range(2)]
        lap = [near[part] - 2.0 * centre[part] for part in range(2)]
        lap_two = [far[part] - 4.0 * near[part] + 6.0 * centre[part] for part in range(2)]
        return (
            centre[0] + COUPLING * lap[1] - half * lap_two[0],
            centre[1] - COUPLING * lap[0] - half * lap_two[1],
        )

    def step(index, first, count, last):
        for q in range(inner):
            for base in range(first, first + count, 8):
                turned = small_dft([couple(p, q, base) for p in range(outer)], -1.0)
                for kp in range(outer):
                    value = times_fixed(turned[kp], -root_angle * q * kp)
                    mid[0, kp, q, base : base + 8] = value[0]
                    mid[1, kp, q, base : base + 8] = value[1]
        for kp in range(outer):
            for base in range(first, first + count, 16):
                at = slice(base, base + 16)
                turned = small_dft([(mid[0, kp, q, at], mid[1, kp, q, at]) for q in range(inner)], -1.0)
                for kq in range(inner):
                    k1 = kp + outer * kq
                    value = times(turned[kq], (tables[0, k1], tables[1, k1]))
                    for part in range(2):
                        lanes = slice(part * LANES, (part + 1) * LANES)
                        head = value[part].astype(jnp.bfloat16)
                        packed = slice(base - first, base - first + 16)
                        high[kp, kq, packed, lanes] = head
                        low[kp, kq, packed, lanes] = (value[part] - head.astype(jnp.float32)).astype(jnp.bfloat16)
        shape = (inner * count, 2 * LANES)
        rng = slice(first, first + count)

        def product(head, tail, table):
            def dot(a, b):
                return lax.dot_general(a, b, (((1,), (0,)), ((), ())), preferred_element_type=jnp.float32)

            return dot(head, table[0]) + dot(tail, table[0]) + dot(head, table[1])

        for kp in range(outer):
            head = high[kp, :, :count].reshape(shape)
            tail = low[kp, :, :count].reshape(shape)
            spec = product(head, tail, ahead)
            spec_re = spec[:, :LANES].reshape(inner, count, LANES)
            spec_im = spec[:, LANES:].reshape(inner, count, LANES)
            phase_c = jnp.stack([tables[2, kp + outer * kq] for kq in range(inner)])
            phase_s = jnp.stack([tables[3, kp + outer * kq] for kq in range(inner)])
            spec_re, spec_im = times((spec_re, spec_im), (phase_c, phase_s))
            spec = jnp.concatenate([spec_re.reshape(shape[0], LANES), spec_im.reshape(shape[0], LANES)], axis=1)
            head = spec.astype(jnp.bfloat16)
            tail = (spec - head.astype(jnp.float32)).astype(jnp.bfloat16)
            spec = product(head, tail, back)
            mid[0, kp, :, rng] = spec[:, :LANES].reshape(inner, count, LANES)
            mid[1, kp, :, rng] = spec[:, LANES:].reshape(inner, count, LANES)
        for kp in range(outer):
            for base in range(first, first + count, 8):
                at = slice(base, base + 8)
                values = []
                for kq in range(inner):
                    k1 = kp + outer * kq
                    values.append(times((mid[0, kp, kq, at], mid[1, kp, kq, at]), (tables[0, k1], -tables[1, k1])))
                turned = small_dft(values, 1.0)
                for q in range(inner):
                    value = times_fixed(turned[q], root_angle * q * kp)
                    mid[0, kp, q, at] = value[0]
                    mid[1, kp, q, at] = value[1]
        for q in range(inner):
            lanes = slice(q * LANES, (q + 1) * LANES)
            for base in range(first, first + count, 8):
                at = slice(base, base + 8)
                turned = small_dft([(mid[0, kp, q, at], mid[1, kp, q, at]) for kp in range(outer)], 1.0)
                for p in range(outer):
                    if halo <= base < halo + own:
                        centre = slice(base - halo, base - halo + 8)
                        for part in range(2):
                            if last:
                                out[p, part, centre, lanes] = turned[p][part]
                            else:
                                past[p, index, part, centre, lanes] = turned[p][part]
                    if not last:
                        turn_screen(turned[p], p, q, base)

    spans = []
    for index in range(steps):
        first = 2 * (index + 1) // 8 * 8
        spans.append((first, rows - 2 * first))
    index = 0
    while index < steps:
        stop = index
        while stop < steps - 1 and spans[stop] == spans[index]:
            stop += 1
        if index == steps - 1:
            step(index, *spans[index], True)
            break
        if stop == index:
            stop = index + 1

        def run(at, carry, span=spans[index]):
            step(at, *span, False)
            return carry

        lax.fori_loop(index, stop, run, 0)
        index = stop


def run_steps(window, steps, halo):
    sources, _, rows, cols = window.shape
    inner = cols // LANES
    ahead, back, tables = transform_tables(sources * cols)
    own = rows - 2 * halo
    vmem = pl.BlockSpec(memory_space=pltpu.VMEM)
    field = (sources, inner)
    return pl.pallas_call(
        lambda *refs: steps_kernel(steps, halo, *refs),
        out_shape=(
            jax.ShapeDtypeStruct((sources, steps - 1, 2, own, cols), jnp.float32),
            jax.ShapeDtypeStruct((sources, 2, own, cols), jnp.float32),
        ),
        in_specs=[vmem] * 4,
        out_specs=(vmem, vmem),
        scratch_shapes=[
            pltpu.VMEM((2,) + field + (rows + 2 * ROW_PAD, LANES), jnp.float32),
            pltpu.VMEM(field + (rows, LANES), jnp.float32),
            pltpu.VMEM(field + (rows, LANES), jnp.float32),
            pltpu.VMEM((2,) + field + (rows, LANES), jnp.float32),
            pltpu.VMEM(field + (rows, 2 * LANES), jnp.bfloat16),
            pltpu.VMEM(field + (rows, 2 * LANES), jnp.bfloat16),
        ],
        compiler_params=pltpu.CompilerParams(vmem_limit_bytes=40 * 1024 * 1024),
        name="steps",
    )(window, jnp.asarray(ahead), jnp.asarray(back), jnp.asarray(tables))


def group_sums(blocks, marks):
    hit = marks[:, :, None] == jnp.arange(GROUPS, dtype=jnp.int32)
    return jnp.sum(jnp.where(hit, blocks[:, :, None], 0.0), axis=(0, 1))


def block_sums(term):
    return term.reshape(term.shape[:-1] + (-1, LABEL_BLOCK)).sum(-1)


def on_device(adjoint_in, forward_field, screen, bed_weight, labels):
    steps = forward_field.shape[0]
    sectors = lax.axis_size("az")
    ranges = lax.axis_size("dep")
    rank = lax.axis_index("dep")
    rows_here, cols_here = screen.shape
    own = rows_here // ranges
    halo = 2 * steps
    blocks_here = cols_here // LABEL_BLOCK

    stacked = jnp.concatenate([adjoint_in, screen[None]])
    ahead = [(i, (i + 1) % sectors) for i in range(sectors)]
    behind = [((i + 1) % sectors, i) for i in range(sectors)]
    above = lax.ppermute(stacked[:, rows_here - halo :], "az", ahead)
    below = lax.ppermute(stacked[:, :halo], "az", behind)
    wide = jnp.concatenate([above, stacked, below], axis=1)
    windows = jnp.stack([wide[:, d * own : (d + 1) * own + 2 * halo] for d in range(ranges)])
    window = lax.all_to_all(windows, "dep", 0, 0)

    stored = forward_field[: steps - 1].reshape(steps - 1, 2, ranges, own, cols_here)
    stored = lax.all_to_all(jnp.transpose(stored, (2, 0, 1, 3, 4)), "dep", 0, 0)

    past, final = run_steps(window, steps, halo)
    field = lax.all_to_all(final, "dep", 0, 0)
    field = jnp.transpose(field, (1, 0, 2, 3)).reshape(2, rows_here, cols_here)

    stored = stored[:, ::-1]
    term = jnp.sum(past[:, :, 1] * stored[:, :, 0] - past[:, :, 0] * stored[:, :, 1], axis=1)
    term = term * bed_weight.reshape(ranges, 1, cols_here)
    marks = lax.dynamic_slice_in_dim(labels, rank * own, own, 0)
    blocks = block_sums(term)
    marks = jnp.transpose(marks.reshape(own, ranges, blocks_here), (1, 0, 2))
    sums = group_sums(blocks.reshape(ranges * own, blocks_here), marks.reshape(ranges * own, blocks_here))

    weight_here = lax.dynamic_slice_in_dim(bed_weight, rank * cols_here, cols_here, 0)
    latest = forward_field[steps - 1]
    here = (adjoint_in[1] * latest[0] - adjoint_in[0] * latest[1]) * weight_here
    marks_here = lax.dynamic_slice_in_dim(labels, rank * blocks_here, blocks_here, 1)
    sums = sums + group_sums(block_sums(here), marks_here)

    sums = jnp.sum(lax.all_to_all(jnp.broadcast_to(sums, (ranges, GROUPS)), "dep", 0, 0), axis=0)
    sums = jnp.sum(lax.all_to_all(jnp.broadcast_to(sums, (sectors, GROUPS)), "az", 0, 0), axis=0)
    return (field, sums)


def solution(mesh):
    return jax.shard_map(
        on_device,
        mesh=mesh,
        in_specs=(
            P(None, "az", "dep"),
            P(None, None, "az", "dep"),
            P("az", "dep"),
            P(),
            P("az", None),
        ),
        out_specs=(P(None, "az", "dep"), P()),
        check_vma=False,
    )
```

```python
import math

import jax
import jax.numpy as jnp
import ml_dtypes
import numpy as np
from jax import lax
from jax.experimental import pallas as pl
from jax.experimental.pallas import tpu as pltpu
from jax.sharding import PartitionSpec as P

GROUPS = 32
COUPLING = 0.15
LABEL_BLOCK = 128
LANES = 128
ROW_PAD = 8
SCALARS = pl.BlockSpec(memory_space=pltpu.SMEM)
IN_PLACE = pl.BlockSpec(memory_space=pltpu.HBM)


def kept_out(value):
    return pltpu.with_memory_space_constraint(value, pltpu.HBM)


def split_table(table):
    high = table.astype(ml_dtypes.bfloat16)
    low = (table - high.astype(np.float64)).astype(ml_dtypes.bfloat16)
    return np.stack([high, low])


def transform_tables(depths):
    blocks = depths // LANES
    lane = np.arange(LANES)
    turn = 2.0 * np.pi * (np.outer(lane, lane) % LANES) / LANES
    cosine, sine = np.cos(turn), np.sin(turn)
    ahead = np.block([[cosine, -sine], [sine, cosine]])
    back = np.block([[cosine, sine], [-sine, cosine]])
    outer = np.arange(blocks)
    twist = 2.0 * np.pi * np.outer(outer, lane) / depths
    freq = outer[:, None] + blocks * lane[None, :]
    freq = np.where(freq < depths // 2, freq, freq - depths)
    beta = 30.0 * (freq / (depths // 2)) ** 2
    tables = np.stack([np.cos(twist), -np.sin(twist), np.cos(beta) / depths, np.sin(beta) / depths])
    return (
        split_table(ahead),
        split_table(back),
        tables[:, :, None, :].astype(np.float32),
    )


def times(value, factor):
    return (value[0] * factor[0] - value[1] * factor[1], value[0] * factor[1] + value[1] * factor[0])


def times_fixed(value, angle):
    c, s = math.cos(angle), math.sin(angle)
    if abs(s) < 1e-12:
        return value if c > 0 else (-value[0], -value[1])
    if abs(c) < 1e-12:
        return (-value[1], value[0]) if s > 0 else (value[1], -value[0])
    if abs(abs(c) - abs(s)) < 1e-12:
        root = math.sqrt(0.5)
        re = value[0] * math.copysign(1, c) - value[1] * math.copysign(1, s)
        im = value[0] * math.copysign(1, s) + value[1] * math.copysign(1, c)
        return (re * root, im * root)
    return (value[0] * c - value[1] * s, value[0] * s + value[1] * c)


def plus(a, b):
    return (a[0] + b[0], a[1] + b[1])


def minus(a, b):
    return (a[0] - b[0], a[1] - b[1])


def small_dft(values, sign):
    count = len(values)
    if count == 1:
        return values
    even = small_dft(values[0::2], sign)
    odd = small_dft(values[1::2], sign)
    odd = [times_fixed(v, sign * 2.0 * math.pi * k / count) for k, v in enumerate(odd)]
    return [plus(e, o) for e, o in zip(even, odd)] + [minus(e, o) for e, o in zip(even, odd)]


def sine_cosine(angle):
    half = 0.5 * angle
    square = half * half
    s = jnp.full_like(square, 1.0 / math.factorial(13))
    for order in (11, 9, 7, 5, 3, 1):
        s = s * square + (-1.0) ** (order // 2) / math.factorial(order)
    s = s * half
    c = jnp.full_like(square, 1.0 / math.factorial(12))
    for order in (10, 8, 6, 4, 2, 0):
        c = c * square + (-1.0) ** (order // 2) / math.factorial(order)
    return 2.0 * s * c, 1.0 - 2.0 * s * s


def steps_kernel(steps, halo, rank, window, ahead_at, back_at, tables_at, past_at, *refs):
    outer = window.shape[0]
    pairs = refs[: outer // 2]
    out, past, scr, angle_c, angle_s, mid, high, low, ahead, back, tables, arrived, left = refs[outer // 2 :]
    copies = [
        pltpu.make_async_copy(source, target, arrived.at[number])
        for number, (source, target) in enumerate(((ahead_at, ahead), (back_at, back), (tables_at, tables)))
    ]
    for copy in copies:
        copy.start()
    inner = mid.shape[2]
    blocks = outer * inner
    rows = window.shape[2]
    own = rows - 2 * halo
    root_angle = 2.0 * math.pi / blocks
    half = 0.5 * COUPLING * COUPLING

    scr[:, :, :, 0:ROW_PAD] = jnp.zeros((2, outer, inner, ROW_PAD, LANES), jnp.float32)
    scr[:, :, :, ROW_PAD + rows :] = jnp.zeros((2, outer, inner, ROW_PAD, LANES), jnp.float32)

    def turn_screen(value, p, q, base):
        c = angle_c[p, q, base : base + 8]
        s = angle_s[p, q, base : base + 8]
        scr[0, p, q, base + ROW_PAD : base + ROW_PAD + 8] = value[0] * c + value[1] * s
        scr[1, p, q, base + ROW_PAD : base + ROW_PAD + 8] = value[1] * c - value[0] * s

    def start(p, carry):
        for q in range(inner):
            lanes = slice(q * LANES, (q + 1) * LANES)
            for base in range(0, rows, 8):
                at = slice(base, base + 8)
                s, c = sine_cosine(window[p, 2, at, lanes])
                angle_c[p, q, at] = c
                angle_s[p, q, at] = s
                turn_screen((window[p, 0, at, lanes], window[p, 1, at, lanes]), p, q, base)
        return carry

    lax.fori_loop(0, outer, start, 0)
    for copy in copies:
        copy.wait()

    def couple(p, q, base):
        def at(part, shift):
            begin = base + ROW_PAD + shift
            return scr[part, p, q, begin : begin + 8]

        centre = [at(part, 0) for part in range(2)]
        near = [at(part, 1) + at(part, -1) for part in range(2)]
        far = [at(part, 2) + at(part, -2) for part in range(2)]
        lap = [near[part] - 2.0 * centre[part] for part in range(2)]
        lap_two = [far[part] - 4.0 * near[part] + 6.0 * centre[part] for part in range(2)]
        return (
            centre[0] + COUPLING * lap[1] - half * lap_two[0],
            centre[1] - COUPLING * lap[0] - half * lap_two[1],
        )

    def step(index, first, count, last):
        for q in range(inner):
            for base in range(first, first + count, 8):
                turned = small_dft([couple(p, q, base) for p in range(outer)], -1.0)
                for kp in range(outer):
                    value = times_fixed(turned[kp], -root_angle * q * kp)
                    mid[0, kp, q, base : base + 8] = value[0]
                    mid[1, kp, q, base : base + 8] = value[1]
        for kp in range(outer):
            for base in range(first, first + count, 16):
                at = slice(base, base + 16)
                turned = small_dft([(mid[0, kp, q, at], mid[1, kp, q, at]) for q in range(inner)], -1.0)
                for kq in range(inner):
                    k1 = kp + outer * kq
                    value = times(turned[kq], (tables[0, k1], tables[1, k1]))
                    for part in range(2):
                        lanes = slice(part * LANES, (part + 1) * LANES)
                        head = value[part].astype(jnp.bfloat16)
                        packed = slice(base - first, base - first + 16)
                        high[kp, kq, packed, lanes] = head
                        low[kp, kq, packed, lanes] = (value[part] - head.astype(jnp.float32)).astype(jnp.bfloat16)
        shape = (inner * count, 2 * LANES)
        rng = slice(first, first + count)

        def product(head, tail, table):
            def dot(a, b):
                return lax.dot_general(a, b, (((1,), (0,)), ((), ())), preferred_element_type=jnp.float32)

            return dot(head, table[0]) + dot(tail, table[0]) + dot(head, table[1])

        for kp in range(outer):
            head = high[kp, :, :count].reshape(shape)
            tail = low[kp, :, :count].reshape(shape)
            spec = product(head, tail, ahead)
            spec_re = spec[:, :LANES].reshape(inner, count, LANES)
            spec_im = spec[:, LANES:].reshape(inner, count, LANES)
            phase_c = jnp.stack([tables[2, kp + outer * kq] for kq in range(inner)])
            phase_s = jnp.stack([tables[3, kp + outer * kq] for kq in range(inner)])
            spec_re, spec_im = times((spec_re, spec_im), (phase_c, phase_s))
            spec = jnp.concatenate([spec_re.reshape(shape[0], LANES), spec_im.reshape(shape[0], LANES)], axis=1)
            head = spec.astype(jnp.bfloat16)
            tail = (spec - head.astype(jnp.float32)).astype(jnp.bfloat16)
            spec = product(head, tail, back)
            mid[0, kp, :, rng] = spec[:, :LANES].reshape(inner, count, LANES)
            mid[1, kp, :, rng] = spec[:, LANES:].reshape(inner, count, LANES)
        for kp in range(outer):
            for base in range(first, first + count, 8):
                at = slice(base, base + 8)
                values = []
                for kq in range(inner):
                    k1 = kp + outer * kq
                    values.append(times((mid[0, kp, kq, at], mid[1, kp, kq, at]), (tables[0, k1], -tables[1, k1])))
                turned = small_dft(values, 1.0)
                for q in range(inner):
                    value = times_fixed(turned[q], root_angle * q * kp)
                    mid[0, kp, q, at] = value[0]
                    mid[1, kp, q, at] = value[1]
        for q in range(inner):
            lanes = slice(q * LANES, (q + 1) * LANES)
            for base in range(first, first + count, 8):
                at = slice(base, base + 8)
                turned = small_dft([(mid[0, kp, q, at], mid[1, kp, q, at]) for kp in range(outer)], 1.0)
                for p in range(outer):
                    if halo <= base < halo + own:
                        centre = slice(base - halo, base - halo + 8)
                        for part in range(2):
                            if last:
                                out[p, part, centre, lanes] = turned[p][part]
                            else:
                                past[index, p, part, centre, lanes] = turned[p][part]
                    if not last:
                        turn_screen(turned[p], p, q, base)

    def leave(at):
        return pltpu.make_async_copy(past.at[at], past_at.at[at], left.at[at])

    spans = []
    for index in range(steps):
        first = 2 * (index + 1) // 8 * 8
        spans.append((first, rows - 2 * first))
    index = 0
    while index < steps:
        stop = index
        while stop < steps - 1 and spans[stop] == spans[index]:
            stop += 1
        if index == steps - 1:
            step(index, *spans[index], True)
            break
        if stop == index:
            stop = index + 1

        def run(at, carry, span=spans[index]):
            step(at, *span, False)
            leave(at).start()
            return carry

        lax.fori_loop(index, stop, run, 0)
        index = stop
    for number, pair in enumerate(pairs):
        for side in range(2):
            pair[side] = out[rank[0] ^ (2 * number + side)]
    for at in range(steps - 1):
        leave(at).wait()


def run_steps(window, rank, steps, halo):
    sources, _, rows, cols = window.shape
    inner = cols // LANES
    ahead, back, tables = transform_tables(sources * cols)
    own = rows - 2 * halo
    vmem = pl.BlockSpec(memory_space=pltpu.VMEM)
    field = (sources, inner)
    result = pl.pallas_call(
        lambda *refs: steps_kernel(steps, halo, *refs),
        out_shape=[pltpu.HBM((steps - 1, sources, 2, own, cols), jnp.float32)]
        + [jax.ShapeDtypeStruct((2, 2, own, cols), jnp.float32)] * (sources // 2),
        in_specs=[SCALARS, vmem] + [IN_PLACE] * 3,
        out_specs=[IN_PLACE] + [vmem] * (sources // 2),
        scratch_shapes=[
            pltpu.VMEM((sources, 2, own, cols), jnp.float32),
            pltpu.VMEM((steps - 1, sources, 2, own, cols), jnp.float32),
            pltpu.VMEM((2,) + field + (rows + 2 * ROW_PAD, LANES), jnp.float32),
            pltpu.VMEM(field + (rows, LANES), jnp.float32),
            pltpu.VMEM(field + (rows, LANES), jnp.float32),
            pltpu.VMEM((2,) + field + (rows, LANES), jnp.float32),
            pltpu.VMEM(field + (rows, 2 * LANES), jnp.bfloat16),
            pltpu.VMEM(field + (rows, 2 * LANES), jnp.bfloat16),
            pltpu.VMEM(ahead.shape, jnp.bfloat16),
            pltpu.VMEM(back.shape, jnp.bfloat16),
            pltpu.VMEM(tables.shape, jnp.float32),
            pltpu.SemaphoreType.DMA((3,)),
            pltpu.SemaphoreType.DMA((steps - 1,)),
        ],
        compiler_params=pltpu.CompilerParams(vmem_limit_bytes=20 * 1024 * 1024),
        cost_estimate=pl.CostEstimate(flops=20_000_000_000, transcendentals=0, bytes_accessed=8_000_000),
        name="steps",
    )(rank, window, *[kept_out(jnp.asarray(table)) for table in (ahead, back, tables)])
    return result[0], result[1:]


def windows_kernel(own, halo, field, screen, above, below, out):
    rows = screen.shape[0]
    for target in range(rows // own):
        first = target * own - halo
        for row in range(first, first + own + 2 * halo, own):
            to = slice(row - first, row - first + own)
            for part in range(3):
                if row < 0:
                    out[target, part, to] = above[part]
                elif row >= rows:
                    out[target, part, to] = below[part]
                elif part < 2:
                    out[target, part, to] = field[part, row : row + own]
                else:
                    out[target, part, to] = screen[row : row + own]


def make_windows(field, screen, above, below, own, halo):
    rows, cols = screen.shape
    vmem = pl.BlockSpec(memory_space=pltpu.VMEM)
    return pl.pallas_call(
        lambda *refs: windows_kernel(own, halo, *refs),
        out_shape=jax.ShapeDtypeStruct((rows // own, 3, own + 2 * halo, cols), jnp.float32),
        in_specs=[vmem] * 4,
        out_specs=vmem,
        compiler_params=pltpu.CompilerParams(vmem_limit_bytes=4 * 1024 * 1024),
        name="windows",
    )(field, screen, above, below)


def add_groups(total, term, marks):
    lane = lax.broadcasted_iota(jnp.int32, total.shape, 1)
    for block in range(term.shape[1] // LABEL_BLOCK):
        part = jnp.sum(term[:, block * LABEL_BLOCK : (block + 1) * LABEL_BLOCK], axis=1, keepdims=True)
        total = total + jnp.where(marks[:, block : block + 1] == lane, part, 0.0)
    return total


def here_kernel(rank, field, latest, weight, marks, out):
    total = jnp.zeros((8, LANES), jnp.float32)
    for row in range(0, field.shape[1], 8):
        at = slice(row, row + 8)
        term = (field[1, at] * latest[0, 0, at] - field[0, at] * latest[0, 1, at]) * weight[rank[0]]
        total = add_groups(total, term, marks[at])
    out[...] = total


def sums_here(rank, field, forward_field, weight, marks):
    steps, _, rows, cols = forward_field.shape
    vmem = pl.BlockSpec(memory_space=pltpu.VMEM)
    return pl.pallas_call(
        here_kernel,
        out_shape=jax.ShapeDtypeStruct((8, LANES), jnp.float32),
        grid=(1,),
        in_specs=[
            SCALARS,
            vmem,
            pl.BlockSpec((1, 2, rows, cols), lambda i: (steps - 1, 0, 0, 0)),
            vmem,
            vmem,
        ],
        out_specs=vmem,
        compiler_params=pltpu.CompilerParams(vmem_limit_bytes=8 * 1024 * 1024),
        cost_estimate=pl.CostEstimate(flops=2_000_000_000, transcendentals=0, bytes_accessed=1_000_000),
        name="here",
    )(rank, field, forward_field, weight, marks)


def sums_kernel(past_at, stored_at, weight, marks, here, out, past, stored, arrived):
    steps, sources, _, own, _ = past.shape
    copies = []
    for source in range(sources):
        copies.append(
            (
                pltpu.make_async_copy(stored_at.at[source], stored.at[source], arrived.at[0, source]),
                pltpu.make_async_copy(past_at.at[:, source], past.at[:, source], arrived.at[1, source]),
            )
        )
    for pair in copies:
        for copy in pair:
            copy.start()
    total = here[...]
    for source, pair in enumerate(copies):
        for copy in pair:
            copy.wait()
        for row in range(0, own, 8):
            at = slice(row, row + 8)
            term = None
            for index in range(steps):
                kept = steps - 1 - index
                one = past[index, source, 1, at] * stored[source, kept, 0, at]
                two = past[index, source, 0, at] * stored[source, kept, 1, at]
                term = one - two if term is None else term + (one - two)
            total = add_groups(total, term * weight[source], marks[source, at])
    out[...] = jnp.sum(total, axis=0, keepdims=True)


def group_sums(past, stored, weight, marks, here):
    vmem = pl.BlockSpec(memory_space=pltpu.VMEM)
    return pl.pallas_call(
        sums_kernel,
        out_shape=jax.ShapeDtypeStruct((1, LANES), jnp.float32),
        in_specs=[IN_PLACE] * 2 + [vmem] * 3,
        out_specs=vmem,
        scratch_shapes=[
            pltpu.VMEM(past.shape, jnp.float32),
            pltpu.VMEM(stored.shape, jnp.float32),
            pltpu.SemaphoreType.DMA((2, past.shape[1])),
        ],
        compiler_params=pltpu.CompilerParams(vmem_limit_bytes=10 * 1024 * 1024),
        name="sums",
    )(kept_out(past), kept_out(stored), weight, marks, here)


def gather_kernel(rank, across, *refs):
    pairs, out = refs[:-1], refs[-1]
    own = across.shape[2]
    for number, pair in enumerate(pairs):
        for side, piece in enumerate((pair[0], across[number])):
            row = pl.multiple_of((rank[0] ^ (2 * number + side)) * own, own)
            out[:, pl.ds(row, own)] = piece


def gather_rows(rank, across, pairs):
    _, _, own, cols = across.shape
    vmem = pl.BlockSpec(memory_space=pltpu.VMEM)
    return pl.pallas_call(
        gather_kernel,
        out_shape=jax.ShapeDtypeStruct((2, 2 * own * len(pairs), cols), jnp.float32),
        in_specs=[SCALARS] + [vmem] * (1 + len(pairs)),
        out_specs=vmem,
        compiler_params=pltpu.CompilerParams(vmem_limit_bytes=8 * 1024 * 1024),
        name="gather",
    )(rank, across, *pairs)


def swap(value, other, count):
    return lax.ppermute(value, "dep", [(i, i ^ other) for i in range(count)])


def on_device(adjoint_in, forward_field, screen, bed_weight, labels):
    steps = forward_field.shape[0]
    sectors = lax.axis_size("az")
    ranges = lax.axis_size("dep")
    position = lax.axis_index("dep")
    rank = position.reshape(1)
    rows_here, cols_here = screen.shape
    own = rows_here // ranges
    halo = 2 * steps
    blocks_here = cols_here // LABEL_BLOCK

    def edge(rows):
        return jnp.concatenate([adjoint_in[:, rows], screen[None, rows]])

    ahead = [(i, (i + 1) % sectors) for i in range(sectors)]
    behind = [((i + 1) % sectors, i) for i in range(sectors)]
    above = lax.ppermute(edge(slice(rows_here - halo, rows_here)), "az", ahead)
    below = lax.ppermute(edge(slice(0, halo)), "az", behind)

    windows = make_windows(adjoint_in, screen, above, below, own, halo)
    window = lax.all_to_all(windows, "dep", 0, 0)

    weight = bed_weight.reshape(ranges, 1, cols_here)
    marks_here = lax.dynamic_slice_in_dim(labels, position * blocks_here, blocks_here, 1)
    here = sums_here(rank, adjoint_in, forward_field, weight, marks_here)
    marks = lax.dynamic_slice_in_dim(labels, position * own, own, 0)
    marks = jnp.transpose(marks.reshape(own, ranges, blocks_here), (1, 0, 2))

    stored = forward_field[: steps - 1].reshape(steps - 1, 2, ranges, own, cols_here)
    stored = jnp.transpose(stored, (2, 0, 1, 3, 4))
    window, here, marks, stored = lax.optimization_barrier((window, here, marks, stored))
    stored = lax.all_to_all(stored, "dep", 0, 0)

    past, pairs = run_steps(window, rank, steps, halo)
    pairs = [pairs[0]] + [swap(pairs[number], 2 * number, ranges) for number in range(1, ranges // 2)]
    sums = group_sums(past, stored, weight, marks, here)
    _, *ready = lax.optimization_barrier((sums, *pairs))
    across = jnp.stack([pair[1] for pair in ready])
    field = gather_rows(rank, swap(across, 1, ranges), ready)
    sums = jnp.broadcast_to(sums[None, 0, :GROUPS], (sectors * ranges, GROUPS))
    sums = jnp.sum(lax.all_to_all(sums, ("az", "dep"), 0, 0), axis=0)
    return (field, sums)


def solution(mesh):
    return jax.shard_map(
        on_device,
        mesh=mesh,
        in_specs=(
            P(None, "az", "dep"),
            P(None, None, "az", "dep"),
            P("az", "dep"),
            P(),
            P("az", None),
        ),
        out_specs=(P(None, "az", "dep"), P()),
        check_vma=False,
    )
```

```python
import math

import jax
import jax.numpy as jnp
import ml_dtypes
import numpy as np
from jax import lax
from jax.experimental import pallas as pl
from jax.experimental.pallas import tpu as pltpu
from jax.sharding import PartitionSpec as P

GROUPS = 32
COUPLING = 0.15
LABEL_BLOCK = 128
LANES = 128
ROW_PAD = 8
SCALARS = pl.BlockSpec(memory_space=pltpu.SMEM)
IN_PLACE = pl.BlockSpec(memory_space=pltpu.HBM)


def kept_out(value):
    return pltpu.with_memory_space_constraint(value, pltpu.HBM)


def split_table(table):
    high = table.astype(ml_dtypes.bfloat16)
    low = (table - high.astype(np.float64)).astype(ml_dtypes.bfloat16)
    return np.stack([high, low])


def transform_tables(depths):
    blocks = depths // LANES
    lane = np.arange(LANES)
    turn = 2.0 * np.pi * (np.outer(lane, lane) % LANES) / LANES
    cosine, sine = np.cos(turn), np.sin(turn)
    ahead = np.block([[cosine, -sine], [sine, cosine]])
    back = np.block([[cosine, sine], [-sine, cosine]])
    outer = np.arange(blocks)
    twist = 2.0 * np.pi * np.outer(outer, lane) / depths
    freq = outer[:, None] + blocks * lane[None, :]
    freq = np.where(freq < depths // 2, freq, freq - depths)
    beta = 30.0 * (freq / (depths // 2)) ** 2
    tables = np.stack([np.cos(twist), -np.sin(twist), np.cos(beta) / depths, np.sin(beta) / depths])
    return (
        split_table(ahead),
        split_table(back),
        tables[:, :, None, :].astype(np.float32),
    )


def times(value, factor):
    return (value[0] * factor[0] - value[1] * factor[1], value[0] * factor[1] + value[1] * factor[0])


def times_fixed(value, angle):
    c, s = math.cos(angle), math.sin(angle)
    if abs(s) < 1e-12:
        return value if c > 0 else (-value[0], -value[1])
    if abs(c) < 1e-12:
        return (-value[1], value[0]) if s > 0 else (value[1], -value[0])
    if abs(abs(c) - abs(s)) < 1e-12:
        root = math.sqrt(0.5)
        re = value[0] * math.copysign(1, c) - value[1] * math.copysign(1, s)
        im = value[0] * math.copysign(1, s) + value[1] * math.copysign(1, c)
        return (re * root, im * root)
    return (value[0] * c - value[1] * s, value[0] * s + value[1] * c)


def plus(a, b):
    return (a[0] + b[0], a[1] + b[1])


def minus(a, b):
    return (a[0] - b[0], a[1] - b[1])


def small_dft(values, sign):
    count = len(values)
    if count == 1:
        return values
    even = small_dft(values[0::2], sign)
    odd = small_dft(values[1::2], sign)
    odd = [times_fixed(v, sign * 2.0 * math.pi * k / count) for k, v in enumerate(odd)]
    return [plus(e, o) for e, o in zip(even, odd)] + [minus(e, o) for e, o in zip(even, odd)]


def sine_cosine(angle):
    half = 0.5 * angle
    square = half * half
    s = jnp.full_like(square, 1.0 / math.factorial(13))
    for order in (11, 9, 7, 5, 3, 1):
        s = s * square + (-1.0) ** (order // 2) / math.factorial(order)
    s = s * half
    c = jnp.full_like(square, 1.0 / math.factorial(12))
    for order in (10, 8, 6, 4, 2, 0):
        c = c * square + (-1.0) ** (order // 2) / math.factorial(order)
    return 2.0 * s * c, 1.0 - 2.0 * s * s


def steps_kernel(steps, halo, rank, window, ahead_at, back_at, tables_at, past_at, *refs):
    outer = window.shape[0]
    pairs = refs[: outer // 2]
    out, past, scr, angle_c, angle_s, mid, high, low, ahead, back, tables, arrived, left = refs[outer // 2 :]
    copies = [
        pltpu.make_async_copy(source, target, arrived.at[number])
        for number, (source, target) in enumerate(((ahead_at, ahead), (back_at, back), (tables_at, tables)))
    ]
    for copy in copies:
        copy.start()
    inner = mid.shape[2]
    blocks = outer * inner
    rows = window.shape[2]
    own = rows - 2 * halo
    root_angle = 2.0 * math.pi / blocks
    half = 0.5 * COUPLING * COUPLING

    scr[:, :, :, 0:ROW_PAD] = jnp.zeros((2, outer, inner, ROW_PAD, LANES), jnp.float32)
    scr[:, :, :, ROW_PAD + rows :] = jnp.zeros((2, outer, inner, ROW_PAD, LANES), jnp.float32)

    def turn_screen(value, p, q, base):
        c = angle_c[p, q, base : base + 8]
        s = angle_s[p, q, base : base + 8]
        scr[0, p, q, base + ROW_PAD : base + ROW_PAD + 8] = value[0] * c + value[1] * s
        scr[1, p, q, base + ROW_PAD : base + ROW_PAD + 8] = value[1] * c - value[0] * s

    def start(p, carry):
        for q in range(inner):
            lanes = slice(q * LANES, (q + 1) * LANES)
            for base in range(0, rows, 8):
                at = slice(base, base + 8)
                s, c = sine_cosine(window[p, 2, at, lanes])
                angle_c[p, q, at] = c
                angle_s[p, q, at] = s
                turn_screen((window[p, 0, at, lanes], window[p, 1, at, lanes]), p, q, base)
        return carry

    lax.fori_loop(0, outer, start, 0)
    for copy in copies:
        copy.wait()

    def couple(p, q, base):
        def at(part, shift):
            begin = base + ROW_PAD + shift
            return scr[part, p, q, begin : begin + 8]

        centre = [at(part, 0) for part in range(2)]
        near = [at(part, 1) + at(part, -1) for part in range(2)]
        far = [at(part, 2) + at(part, -2) for part in range(2)]
        lap = [near[part] - 2.0 * centre[part] for part in range(2)]
        lap_two = [far[part] - 4.0 * near[part] + 6.0 * centre[part] for part in range(2)]
        return (
            centre[0] + COUPLING * lap[1] - half * lap_two[0],
            centre[1] - COUPLING * lap[0] - half * lap_two[1],
        )

    def step(index, first, count, last):
        for q in range(inner):
            for base in range(first, first + count, 8):
                turned = small_dft([couple(p, q, base) for p in range(outer)], -1.0)
                for kp in range(outer):
                    value = times_fixed(turned[kp], -root_angle * q * kp)
                    mid[0, kp, q, base : base + 8] = value[0]
                    mid[1, kp, q, base : base + 8] = value[1]
        for kp in range(outer):
            for base in range(first, first + count, 16):
                at = slice(base, base + 16)
                turned = small_dft([(mid[0, kp, q, at], mid[1, kp, q, at]) for q in range(inner)], -1.0)
                for kq in range(inner):
                    k1 = kp + outer * kq
                    value = times(turned[kq], (tables[0, k1], tables[1, k1]))
                    for part in range(2):
                        lanes = slice(part * LANES, (part + 1) * LANES)
                        head = value[part].astype(jnp.bfloat16)
                        packed = slice(base - first, base - first + 16)
                        high[kp, kq, packed, lanes] = head
                        low[kp, kq, packed, lanes] = (value[part] - head.astype(jnp.float32)).astype(jnp.bfloat16)
        shape = (inner * count, 2 * LANES)
        rng = slice(first, first + count)

        def product(head, tail, table):
            def dot(a, b):
                return lax.dot_general(a, b, (((1,), (0,)), ((), ())), preferred_element_type=jnp.float32)

            return dot(head, table[0]) + dot(tail, table[0]) + dot(head, table[1])

        for kp in range(outer):
            head = high[kp, :, :count].reshape(shape)
            tail = low[kp, :, :count].reshape(shape)
            spec = product(head, tail, ahead)
            spec_re = spec[:, :LANES].reshape(inner, count, LANES)
            spec_im = spec[:, LANES:].reshape(inner, count, LANES)
            phase_c = jnp.stack([tables[2, kp + outer * kq] for kq in range(inner)])
            phase_s = jnp.stack([tables[3, kp + outer * kq] for kq in range(inner)])
            spec_re, spec_im = times((spec_re, spec_im), (phase_c, phase_s))
            spec = jnp.concatenate([spec_re.reshape(shape[0], LANES), spec_im.reshape(shape[0], LANES)], axis=1)
            head = spec.astype(jnp.bfloat16)
            tail = (spec - head.astype(jnp.float32)).astype(jnp.bfloat16)
            spec = product(head, tail, back)
            mid[0, kp, :, rng] = spec[:, :LANES].reshape(inner, count, LANES)
            mid[1, kp, :, rng] = spec[:, LANES:].reshape(inner, count, LANES)
        for kp in range(outer):
            for base in range(first, first + count, 8):
                at = slice(base, base + 8)
                values = []
                for kq in range(inner):
                    k1 = kp + outer * kq
                    values.append(times((mid[0, kp, kq, at], mid[1, kp, kq, at]), (tables[0, k1], -tables[1, k1])))
                turned = small_dft(values, 1.0)
                for q in range(inner):
                    value = times_fixed(turned[q], root_angle * q * kp)
                    mid[0, kp, q, at] = value[0]
                    mid[1, kp, q, at] = value[1]
        for q in range(inner):
            lanes = slice(q * LANES, (q + 1) * LANES)
            for base in range(first, first + count, 8):
                at = slice(base, base + 8)
                turned = small_dft([(mid[0, kp, q, at], mid[1, kp, q, at]) for kp in range(outer)], 1.0)
                for p in range(outer):
                    if halo <= base < halo + own:
                        centre = slice(base - halo, base - halo + 8)
                        for part in range(2):
                            if last:
                                out[p, part, centre, lanes] = turned[p][part]
                            else:
                                past[index, p, part, centre, lanes] = turned[p][part]
                    if not last:
                        turn_screen(turned[p], p, q, base)

    def leave(at):
        return pltpu.make_async_copy(past.at[at], past_at.at[at], left.at[at])

    spans = []
    for index in range(steps):
        first = 2 * (index + 1) // 8 * 8
        spans.append((first, rows - 2 * first))
    index = 0
    while index < steps:
        stop = index
        while stop < steps - 1 and spans[stop] == spans[index]:
            stop += 1
        if index == steps - 1:
            step(index, *spans[index], True)
            break
        if stop == index:
            stop = index + 1

        def run(at, carry, span=spans[index]):
            step(at, *span, False)
            leave(at).start()
            return carry

        lax.fori_loop(index, stop, run, 0)
        index = stop
    for number, pair in enumerate(pairs):
        for side in range(2):
            pair[side] = out[rank[0] ^ (2 * number + side)]
    for at in range(steps - 1):
        leave(at).wait()


def run_steps(window, rank, steps, halo):
    sources, _, rows, cols = window.shape
    inner = cols // LANES
    ahead, back, tables = transform_tables(sources * cols)
    own = rows - 2 * halo
    vmem = pl.BlockSpec(memory_space=pltpu.VMEM)
    field = (sources, inner)
    result = pl.pallas_call(
        lambda *refs: steps_kernel(steps, halo, *refs),
        out_shape=[pltpu.HBM((steps - 1, sources, 2, own, cols), jnp.float32)]
        + [jax.ShapeDtypeStruct((2, 2, own, cols), jnp.float32)] * (sources // 2),
        in_specs=[SCALARS, vmem] + [IN_PLACE] * 3,
        out_specs=[IN_PLACE] + [vmem] * (sources // 2),
        scratch_shapes=[
            pltpu.VMEM((sources, 2, own, cols), jnp.float32),
            pltpu.VMEM((steps - 1, sources, 2, own, cols), jnp.float32),
            pltpu.VMEM((2,) + field + (rows + 2 * ROW_PAD, LANES), jnp.float32),
            pltpu.VMEM(field + (rows, LANES), jnp.float32),
            pltpu.VMEM(field + (rows, LANES), jnp.float32),
            pltpu.VMEM((2,) + field + (rows, LANES), jnp.float32),
            pltpu.VMEM(field + (rows, 2 * LANES), jnp.bfloat16),
            pltpu.VMEM(field + (rows, 2 * LANES), jnp.bfloat16),
            pltpu.VMEM(ahead.shape, jnp.bfloat16),
            pltpu.VMEM(back.shape, jnp.bfloat16),
            pltpu.VMEM(tables.shape, jnp.float32),
            pltpu.SemaphoreType.DMA((3,)),
            pltpu.SemaphoreType.DMA((steps - 1,)),
        ],
        compiler_params=pltpu.CompilerParams(vmem_limit_bytes=20 * 1024 * 1024),
        cost_estimate=pl.CostEstimate(flops=20_000_000_000, transcendentals=0, bytes_accessed=8_000_000),
        name="steps",
    )(rank, window, *[kept_out(jnp.asarray(table)) for table in (ahead, back, tables)])
    return result[0], result[1:]


def edges_kernel(halo, field, screen, held, top, bottom, arrived):
    rows = held.shape[1]
    copies = [
        pltpu.make_async_copy(field, held.at[0:2], arrived.at[0]),
        pltpu.make_async_copy(screen, held.at[2], arrived.at[1]),
    ]
    for copy in copies:
        copy.start()
    for copy in copies:
        copy.wait()
    top[...] = held[:, 0:halo]
    bottom[...] = held[:, rows - halo : rows]


def take_edges(field, screen, halo):
    rows, cols = screen.shape
    vmem = pl.BlockSpec(memory_space=pltpu.VMEM)
    return pl.pallas_call(
        lambda *refs: edges_kernel(halo, *refs),
        out_shape=[jax.ShapeDtypeStruct((3, count, cols), jnp.float32) for count in (rows, halo, halo)],
        in_specs=[IN_PLACE] * 2,
        out_specs=[vmem] * 3,
        scratch_shapes=[pltpu.SemaphoreType.DMA((2,))],
        compiler_params=pltpu.CompilerParams(vmem_limit_bytes=4 * 1024 * 1024),
        name="edges",
    )(kept_out(field), kept_out(screen))


def windows_kernel(own, halo, sector, above, below, out):
    rows = sector.shape[1]
    for target in range(rows // own):
        first = target * own - halo
        low = max(first, 0)
        high = min(first + own + 2 * halo, rows)
        out[target, :, low - first : high - first] = sector[:, low:high]
        if low > first:
            out[target, :, : low - first] = above[...]
        if high < first + own + 2 * halo:
            out[target, :, high - first :] = below[...]


def make_windows(sector, above, below, own, halo):
    _, rows, cols = sector.shape
    vmem = pl.BlockSpec(memory_space=pltpu.VMEM)
    return pl.pallas_call(
        lambda *refs: windows_kernel(own, halo, *refs),
        out_shape=jax.ShapeDtypeStruct((rows // own, 3, own + 2 * halo, cols), jnp.float32),
        in_specs=[vmem] * 3,
        out_specs=vmem,
        compiler_params=pltpu.CompilerParams(vmem_limit_bytes=4 * 1024 * 1024),
        name="windows",
    )(sector, above, below)


def add_groups(total, term, marks):
    lane = lax.broadcasted_iota(jnp.int32, total.shape, 1)
    for block in range(term.shape[1] // LABEL_BLOCK):
        part = jnp.sum(term[:, block * LABEL_BLOCK : (block + 1) * LABEL_BLOCK], axis=1, keepdims=True)
        total = total + jnp.where(marks[:, block : block + 1] == lane, part, 0.0)
    return total


def here_kernel(rank, field, latest, weight, marks, out):
    total = jnp.zeros((8, LANES), jnp.float32)
    for row in range(0, field.shape[1], 8):
        at = slice(row, row + 8)
        term = (field[1, at] * latest[0, 0, at] - field[0, at] * latest[0, 1, at]) * weight[rank[0]]
        total = add_groups(total, term, marks[at])
    out[...] = total


def sums_here(rank, field, forward_field, weight, marks):
    steps, _, rows, cols = forward_field.shape
    vmem = pl.BlockSpec(memory_space=pltpu.VMEM)
    return pl.pallas_call(
        here_kernel,
        out_shape=jax.ShapeDtypeStruct((8, LANES), jnp.float32),
        grid=(1,),
        in_specs=[
            SCALARS,
            vmem,
            pl.BlockSpec((1, 2, rows, cols), lambda i: (steps - 1, 0, 0, 0)),
            vmem,
            vmem,
        ],
        out_specs=vmem,
        compiler_params=pltpu.CompilerParams(vmem_limit_bytes=8 * 1024 * 1024),
        cost_estimate=pl.CostEstimate(flops=2_000_000_000, transcendentals=0, bytes_accessed=1_000_000),
        name="here",
    )(rank, field, forward_field, weight, marks)


def sums_kernel(past_at, stored_at, weight, marks, here, out, past, stored, arrived):
    steps, sources, _, own, _ = past.shape
    copies = []
    for source in range(sources):
        copies.append(
            (
                pltpu.make_async_copy(stored_at.at[source], stored.at[source], arrived.at[0, source]),
                pltpu.make_async_copy(past_at.at[:, source], past.at[:, source], arrived.at[1, source]),
            )
        )
    for pair in copies:
        for copy in pair:
            copy.start()
    total = here[...]
    for source, pair in enumerate(copies):
        for copy in pair:
            copy.wait()
        for row in range(0, own, 8):
            at = slice(row, row + 8)
            term = None
            for index in range(steps):
                kept = steps - 1 - index
                one = past[index, source, 1, at] * stored[source, kept, 0, at]
                two = past[index, source, 0, at] * stored[source, kept, 1, at]
                term = one - two if term is None else term + (one - two)
            total = add_groups(total, term * weight[source], marks[source, at])
    out[...] = jnp.sum(total, axis=0, keepdims=True)


def group_sums(past, stored, weight, marks, here):
    vmem = pl.BlockSpec(memory_space=pltpu.VMEM)
    return pl.pallas_call(
        sums_kernel,
        out_shape=jax.ShapeDtypeStruct((1, LANES), jnp.float32),
        in_specs=[IN_PLACE] * 2 + [vmem] * 3,
        out_specs=vmem,
        scratch_shapes=[
            pltpu.VMEM(past.shape, jnp.float32),
            pltpu.VMEM(stored.shape, jnp.float32),
            pltpu.SemaphoreType.DMA((2, past.shape[1])),
        ],
        compiler_params=pltpu.CompilerParams(vmem_limit_bytes=10 * 1024 * 1024),
        name="sums",
    )(kept_out(past), kept_out(stored), weight, marks, here)


def gather_kernel(rank, across, *refs):
    pairs, out = refs[:-1], refs[-1]
    own = across.shape[2]
    for number, pair in enumerate(pairs):
        for side, piece in enumerate((pair[0], across[number])):
            row = pl.multiple_of((rank[0] ^ (2 * number + side)) * own, own)
            out[:, pl.ds(row, own)] = piece


def gather_rows(rank, across, pairs):
    _, _, own, cols = across.shape
    vmem = pl.BlockSpec(memory_space=pltpu.VMEM)
    return pl.pallas_call(
        gather_kernel,
        out_shape=jax.ShapeDtypeStruct((2, 2 * own * len(pairs), cols), jnp.float32),
        in_specs=[SCALARS] + [vmem] * (1 + len(pairs)),
        out_specs=vmem,
        compiler_params=pltpu.CompilerParams(vmem_limit_bytes=8 * 1024 * 1024),
        name="gather",
    )(rank, across, *pairs)


def swap(value, other, count):
    return lax.ppermute(value, "dep", [(i, i ^ other) for i in range(count)])


def on_device(adjoint_in, forward_field, screen, bed_weight, labels):
    steps = forward_field.shape[0]
    sectors = lax.axis_size("az")
    ranges = lax.axis_size("dep")
    position = lax.axis_index("dep")
    rank = position.reshape(1)
    rows_here, cols_here = screen.shape
    own = rows_here // ranges
    halo = 2 * steps
    blocks_here = cols_here // LABEL_BLOCK

    sector, top, bottom = take_edges(adjoint_in, screen, halo)
    ahead = [(i, (i + 1) % sectors) for i in range(sectors)]
    behind = [((i + 1) % sectors, i) for i in range(sectors)]
    above = lax.ppermute(bottom, "az", ahead)
    below = lax.ppermute(top, "az", behind)

    windows = make_windows(sector, above, below, own, halo)
    window = lax.all_to_all(windows, "dep", 0, 0)

    weight = bed_weight.reshape(ranges, 1, cols_here)
    marks_here = lax.dynamic_slice_in_dim(labels, position * blocks_here, blocks_here, 1)
    here = sums_here(rank, adjoint_in, forward_field, weight, marks_here)
    marks = lax.dynamic_slice_in_dim(labels, position * own, own, 0)
    marks = jnp.transpose(marks.reshape(own, ranges, blocks_here), (1, 0, 2))

    stored = forward_field[: steps - 1].reshape(steps - 1, 2, ranges, own, cols_here)
    stored = jnp.transpose(stored, (2, 0, 1, 3, 4))
    window, here, marks, stored = lax.optimization_barrier((window, here, marks, stored))
    stored = lax.all_to_all(stored, "dep", 0, 0)

    past, pairs = run_steps(window, rank, steps, halo)
    pairs = [pairs[0]] + [swap(pairs[number], 2 * number, ranges) for number in range(1, ranges // 2)]
    sums = group_sums(past, stored, weight, marks, here)
    _, *ready = lax.optimization_barrier((sums, *pairs))
    across = jnp.stack([pair[1] for pair in ready])
    field = gather_rows(rank, swap(across, 1, ranges), ready)
    sums = jnp.broadcast_to(sums[None, 0, :GROUPS], (sectors * ranges, GROUPS))
    sums, field = lax.optimization_barrier((lax.all_to_all(sums, ("az", "dep"), 0, 0), field))
    sums = jnp.sum(sums, axis=0)
    return (field, sums)


def solution(mesh):
    return jax.shard_map(
        on_device,
        mesh=mesh,
        in_specs=(
            P(None, "az", "dep"),
            P(None, None, "az", "dep"),
            P("az", "dep"),
            P(),
            P("az", None),
        ),
        out_specs=(P(None, "az", "dep"), P()),
        check_vma=False,
    )
```

```python
import math

import jax
import jax.numpy as jnp
import ml_dtypes
import numpy as np
from jax import lax
from jax.experimental import pallas as pl
from jax.experimental.pallas import tpu as pltpu
from jax.sharding import PartitionSpec as P

GROUPS = 32
COUPLING = 0.15
LABEL_BLOCK = 128
LANES = 128
ROW_PAD = 8
SCALARS = pl.BlockSpec(memory_space=pltpu.SMEM)
IN_PLACE = pl.BlockSpec(memory_space=pltpu.HBM)


def kept_out(value):
    return pltpu.with_memory_space_constraint(value, pltpu.HBM)


def split_table(table):
    high = table.astype(ml_dtypes.bfloat16)
    low = (table - high.astype(np.float64)).astype(ml_dtypes.bfloat16)
    return np.stack([high, low])


def transform_tables(depths):
    blocks = depths // LANES
    lane = np.arange(LANES)
    turn = 2.0 * np.pi * (np.outer(lane, lane) % LANES) / LANES
    cosine, sine = np.cos(turn), np.sin(turn)
    ahead = np.block([[cosine, -sine], [sine, cosine]])
    back = np.block([[cosine, sine], [-sine, cosine]])
    outer = np.arange(blocks)
    twist = 2.0 * np.pi * np.outer(outer, lane) / depths
    freq = outer[:, None] + blocks * lane[None, :]
    freq = np.where(freq < depths // 2, freq, freq - depths)
    beta = 30.0 * (freq / (depths // 2)) ** 2
    tables = np.stack([np.cos(twist), -np.sin(twist), np.cos(beta) / depths, np.sin(beta) / depths])
    return (
        split_table(ahead),
        split_table(back),
        tables[:, :, None, :].astype(np.float32),
    )


def times(value, factor):
    return (value[0] * factor[0] - value[1] * factor[1], value[0] * factor[1] + value[1] * factor[0])


def times_fixed(value, angle):
    c, s = math.cos(angle), math.sin(angle)
    if abs(s) < 1e-12:
        return value if c > 0 else (-value[0], -value[1])
    if abs(c) < 1e-12:
        return (-value[1], value[0]) if s > 0 else (value[1], -value[0])
    if abs(abs(c) - abs(s)) < 1e-12:
        root = math.sqrt(0.5)
        re = value[0] * math.copysign(1, c) - value[1] * math.copysign(1, s)
        im = value[0] * math.copysign(1, s) + value[1] * math.copysign(1, c)
        return (re * root, im * root)
    return (value[0] * c - value[1] * s, value[0] * s + value[1] * c)


def plus(a, b):
    return (a[0] + b[0], a[1] + b[1])


def minus(a, b):
    return (a[0] - b[0], a[1] - b[1])


def small_dft(values, sign):
    count = len(values)
    if count == 1:
        return values
    even = small_dft(values[0::2], sign)
    odd = small_dft(values[1::2], sign)
    odd = [times_fixed(v, sign * 2.0 * math.pi * k / count) for k, v in enumerate(odd)]
    return [plus(e, o) for e, o in zip(even, odd)] + [minus(e, o) for e, o in zip(even, odd)]


def sine_cosine(angle):
    half = 0.5 * angle
    square = half * half
    s = jnp.full_like(square, 1.0 / math.factorial(13))
    for order in (11, 9, 7, 5, 3, 1):
        s = s * square + (-1.0) ** (order // 2) / math.factorial(order)
    s = s * half
    c = jnp.full_like(square, 1.0 / math.factorial(12))
    for order in (10, 8, 6, 4, 2, 0):
        c = c * square + (-1.0) ** (order // 2) / math.factorial(order)
    return 2.0 * s * c, 1.0 - 2.0 * s * s


def steps_kernel(steps, halo, rank, window, ahead_at, back_at, tables_at, past_at, *refs):
    outer = window.shape[0]
    pairs = refs[: outer // 2]
    out, past, scr, angle_c, angle_s, mid, high, low, ahead, back, tables, arrived, left = refs[outer // 2 :]
    copies = [
        pltpu.make_async_copy(source, target, arrived.at[number])
        for number, (source, target) in enumerate(((ahead_at, ahead), (back_at, back), (tables_at, tables)))
    ]
    for copy in copies:
        copy.start()
    inner = mid.shape[2]
    blocks = outer * inner
    rows = window.shape[2]
    own = rows - 2 * halo
    root_angle = 2.0 * math.pi / blocks
    half = 0.5 * COUPLING * COUPLING

    scr[:, :, :, 0:ROW_PAD] = jnp.zeros((2, outer, inner, ROW_PAD, LANES), jnp.float32)
    scr[:, :, :, ROW_PAD + rows :] = jnp.zeros((2, outer, inner, ROW_PAD, LANES), jnp.float32)

    def turn_screen(value, p, q, base):
        c = angle_c[p, q, base : base + 8]
        s = angle_s[p, q, base : base + 8]
        scr[0, p, q, base + ROW_PAD : base + ROW_PAD + 8] = value[0] * c + value[1] * s
        scr[1, p, q, base + ROW_PAD : base + ROW_PAD + 8] = value[1] * c - value[0] * s

    def start(p, carry):
        for q in range(inner):
            lanes = slice(q * LANES, (q + 1) * LANES)
            for base in range(0, rows, 8):
                at = slice(base, base + 8)
                s, c = sine_cosine(window[p, 2, at, lanes])
                angle_c[p, q, at] = c
                angle_s[p, q, at] = s
                turn_screen((window[p, 0, at, lanes], window[p, 1, at, lanes]), p, q, base)
        return carry

    lax.fori_loop(0, outer, start, 0)
    for copy in copies:
        copy.wait()

    def couple(p, q, base):
        def at(part, shift):
            begin = base + ROW_PAD + shift
            return scr[part, p, q, begin : begin + 8]

        centre = [at(part, 0) for part in range(2)]
        near = [at(part, 1) + at(part, -1) for part in range(2)]
        far = [at(part, 2) + at(part, -2) for part in range(2)]
        lap = [near[part] - 2.0 * centre[part] for part in range(2)]
        lap_two = [far[part] - 4.0 * near[part] + 6.0 * centre[part] for part in range(2)]
        return (
            centre[0] + COUPLING * lap[1] - half * lap_two[0],
            centre[1] - COUPLING * lap[0] - half * lap_two[1],
        )

    def step(index, first, count, last):
        for q in range(inner):
            for base in range(first, first + count, 8):
                turned = small_dft([couple(p, q, base) for p in range(outer)], -1.0)
                for kp in range(outer):
                    value = times_fixed(turned[kp], -root_angle * q * kp)
                    mid[0, kp, q, base : base + 8] = value[0]
                    mid[1, kp, q, base : base + 8] = value[1]
        for kp in range(outer):
            for base in range(first, first + count, 16):
                at = slice(base, base + 16)
                turned = small_dft([(mid[0, kp, q, at], mid[1, kp, q, at]) for q in range(inner)], -1.0)
                for kq in range(inner):
                    k1 = kp + outer * kq
                    value = times(turned[kq], (tables[0, k1], tables[1, k1]))
                    for part in range(2):
                        lanes = slice(part * LANES, (part + 1) * LANES)
                        head = value[part].astype(jnp.bfloat16)
                        packed = slice(base - first, base - first + 16)
                        high[kp, kq, packed, lanes] = head
                        low[kp, kq, packed, lanes] = (value[part] - head.astype(jnp.float32)).astype(jnp.bfloat16)
        shape = (inner * count, 2 * LANES)
        rng = slice(first, first + count)

        def product(head, tail, table):
            def dot(a, b):
                return lax.dot_general(a, b, (((1,), (0,)), ((), ())), preferred_element_type=jnp.float32)

            return dot(head, table[0]) + dot(tail, table[0]) + dot(head, table[1])

        for kp in range(outer):
            head = high[kp, :, :count].reshape(shape)
            tail = low[kp, :, :count].reshape(shape)
            spec = product(head, tail, ahead)
            spec_re = spec[:, :LANES].reshape(inner, count, LANES)
            spec_im = spec[:, LANES:].reshape(inner, count, LANES)
            phase_c = jnp.stack([tables[2, kp + outer * kq] for kq in range(inner)])
            phase_s = jnp.stack([tables[3, kp + outer * kq] for kq in range(inner)])
            spec_re, spec_im = times((spec_re, spec_im), (phase_c, phase_s))
            spec = jnp.concatenate([spec_re.reshape(shape[0], LANES), spec_im.reshape(shape[0], LANES)], axis=1)
            head = spec.astype(jnp.bfloat16)
            tail = (spec - head.astype(jnp.float32)).astype(jnp.bfloat16)
            spec = product(head, tail, back)
            mid[0, kp, :, rng] = spec[:, :LANES].reshape(inner, count, LANES)
            mid[1, kp, :, rng] = spec[:, LANES:].reshape(inner, count, LANES)
        for kp in range(outer):
            for base in range(first, first + count, 8):
                at = slice(base, base + 8)
                values = []
                for kq in range(inner):
                    k1 = kp + outer * kq
                    values.append(times((mid[0, kp, kq, at], mid[1, kp, kq, at]), (tables[0, k1], -tables[1, k1])))
                turned = small_dft(values, 1.0)
                for q in range(inner):
                    value = times_fixed(turned[q], root_angle * q * kp)
                    mid[0, kp, q, at] = value[0]
                    mid[1, kp, q, at] = value[1]
        for q in range(inner):
            lanes = slice(q * LANES, (q + 1) * LANES)
            for base in range(first, first + count, 8):
                at = slice(base, base + 8)
                turned = small_dft([(mid[0, kp, q, at], mid[1, kp, q, at]) for kp in range(outer)], 1.0)
                for p in range(outer):
                    if halo <= base < halo + own:
                        centre = slice(base - halo, base - halo + 8)
                        for part in range(2):
                            if last:
                                out[p, part, centre, lanes] = turned[p][part]
                            else:
                                past[index, p, part, centre, lanes] = turned[p][part]
                    if not last:
                        turn_screen(turned[p], p, q, base)

    def leave(at):
        return pltpu.make_async_copy(past.at[at], past_at.at[:, at], left.at[at])

    spans = []
    for index in range(steps):
        first = 2 * (index + 1) // 8 * 8
        spans.append((first, rows - 2 * first))
    index = 0
    while index < steps:
        stop = index
        while stop < steps - 1 and spans[stop] == spans[index]:
            stop += 1
        if index == steps - 1:
            step(index, *spans[index], True)
            break
        if stop == index:
            stop = index + 1

        def run(at, carry, span=spans[index]):
            step(at, *span, False)
            leave(at).start()
            return carry

        lax.fori_loop(index, stop, run, 0)
        index = stop
    for number, pair in enumerate(pairs):
        for side in range(2):
            pair[side] = out[rank[0] ^ (2 * number + side)]
    for at in range(steps - 1):
        leave(at).wait()


def run_steps(window, rank, steps, halo):
    sources, _, rows, cols = window.shape
    inner = cols // LANES
    ahead, back, tables = transform_tables(sources * cols)
    own = rows - 2 * halo
    vmem = pl.BlockSpec(memory_space=pltpu.VMEM)
    field = (sources, inner)
    result = pl.pallas_call(
        lambda *refs: steps_kernel(steps, halo, *refs),
        out_shape=[pltpu.HBM((sources, steps - 1, 2, own, cols), jnp.float32)]
        + [jax.ShapeDtypeStruct((2, 2, own, cols), jnp.float32)] * (sources // 2),
        in_specs=[SCALARS, vmem] + [IN_PLACE] * 3,
        out_specs=[IN_PLACE] + [vmem] * (sources // 2),
        scratch_shapes=[
            pltpu.VMEM((sources, 2, own, cols), jnp.float32),
            pltpu.VMEM((steps - 1, sources, 2, own, cols), jnp.float32),
            pltpu.VMEM((2,) + field + (rows + 2 * ROW_PAD, LANES), jnp.float32),
            pltpu.VMEM(field + (rows, LANES), jnp.float32),
            pltpu.VMEM(field + (rows, LANES), jnp.float32),
            pltpu.VMEM((2,) + field + (rows, LANES), jnp.float32),
            pltpu.VMEM(field + (rows, 2 * LANES), jnp.bfloat16),
            pltpu.VMEM(field + (rows, 2 * LANES), jnp.bfloat16),
            pltpu.VMEM(ahead.shape, jnp.bfloat16),
            pltpu.VMEM(back.shape, jnp.bfloat16),
            pltpu.VMEM(tables.shape, jnp.float32),
            pltpu.SemaphoreType.DMA((3,)),
            pltpu.SemaphoreType.DMA((steps - 1,)),
        ],
        compiler_params=pltpu.CompilerParams(vmem_limit_bytes=20 * 1024 * 1024),
        cost_estimate=pl.CostEstimate(flops=20_000_000_000, transcendentals=0, bytes_accessed=8_000_000),
        name="steps",
    )(rank, window, *[kept_out(jnp.asarray(table)) for table in (ahead, back, tables)])
    return result[0], result[1:]


def edges_kernel(halo, field, screen, held, top, bottom, arrived):
    rows = held.shape[1]
    copies = [
        pltpu.make_async_copy(field, held.at[0:2], arrived.at[0]),
        pltpu.make_async_copy(screen, held.at[2], arrived.at[1]),
    ]
    for copy in copies:
        copy.start()
    for copy in copies:
        copy.wait()
    top[...] = held[:, 0:halo]
    bottom[...] = held[:, rows - halo : rows]


def take_edges(field, screen, halo):
    rows, cols = screen.shape
    vmem = pl.BlockSpec(memory_space=pltpu.VMEM)
    return pl.pallas_call(
        lambda *refs: edges_kernel(halo, *refs),
        out_shape=[jax.ShapeDtypeStruct((3, count, cols), jnp.float32) for count in (rows, halo, halo)],
        in_specs=[IN_PLACE] * 2,
        out_specs=[vmem] * 3,
        scratch_shapes=[pltpu.SemaphoreType.DMA((2,))],
        compiler_params=pltpu.CompilerParams(vmem_limit_bytes=4 * 1024 * 1024),
        name="edges",
    )(kept_out(field), kept_out(screen))


def windows_kernel(own, halo, sector, above, below, out):
    rows = sector.shape[1]
    for target in range(rows // own):
        first = target * own - halo
        low = max(first, 0)
        high = min(first + own + 2 * halo, rows)
        out[target, :, low - first : high - first] = sector[:, low:high]
        if low > first:
            out[target, :, : low - first] = above[...]
        if high < first + own + 2 * halo:
            out[target, :, high - first :] = below[...]


def make_windows(sector, above, below, own, halo):
    _, rows, cols = sector.shape
    vmem = pl.BlockSpec(memory_space=pltpu.VMEM)
    return pl.pallas_call(
        lambda *refs: windows_kernel(own, halo, *refs),
        out_shape=jax.ShapeDtypeStruct((rows // own, 3, own + 2 * halo, cols), jnp.float32),
        in_specs=[vmem] * 3,
        out_specs=vmem,
        compiler_params=pltpu.CompilerParams(vmem_limit_bytes=4 * 1024 * 1024),
        name="windows",
    )(sector, above, below)


def add_groups(total, term, marks):
    lane = lax.broadcasted_iota(jnp.int32, total.shape, 1)
    for block in range(term.shape[1] // LABEL_BLOCK):
        part = jnp.sum(term[:, block * LABEL_BLOCK : (block + 1) * LABEL_BLOCK], axis=1, keepdims=True)
        total = total + jnp.where(marks[:, block : block + 1] == lane, part, 0.0)
    return total


def here_kernel(rank, field, latest, weight, marks, out):
    total = jnp.zeros((8, LANES), jnp.float32)
    for row in range(0, field.shape[1], 8):
        at = slice(row, row + 8)
        term = (field[1, at] * latest[0, 0, at] - field[0, at] * latest[0, 1, at]) * weight[rank[0]]
        total = add_groups(total, term, marks[at])
    out[...] = total


def sums_here(rank, field, forward_field, weight, marks):
    steps, _, rows, cols = forward_field.shape
    vmem = pl.BlockSpec(memory_space=pltpu.VMEM)
    return pl.pallas_call(
        here_kernel,
        out_shape=jax.ShapeDtypeStruct((8, LANES), jnp.float32),
        grid=(1,),
        in_specs=[
            SCALARS,
            vmem,
            pl.BlockSpec((1, 2, rows, cols), lambda i: (steps - 1, 0, 0, 0)),
            vmem,
            vmem,
        ],
        out_specs=vmem,
        compiler_params=pltpu.CompilerParams(vmem_limit_bytes=8 * 1024 * 1024),
        cost_estimate=pl.CostEstimate(flops=2_000_000_000, transcendentals=0, bytes_accessed=1_000_000),
        name="here",
    )(rank, field, forward_field, weight, marks)


def sums_kernel(past_at, stored_at, weight, marks, here, out, past, stored, arrived):
    sources, steps, _, own, _ = past.shape
    copies = []
    for source in range(sources):
        copies.append(
            (
                pltpu.make_async_copy(stored_at.at[source], stored.at[source], arrived.at[0, source]),
                pltpu.make_async_copy(past_at.at[source], past.at[source], arrived.at[1, source]),
            )
        )
    for pair in copies:
        for copy in pair:
            copy.start()
    total = here[...]
    for source, pair in enumerate(copies):
        for copy in pair:
            copy.wait()
        for row in range(0, own, 8):
            at = slice(row, row + 8)
            term = None
            for index in range(steps):
                kept = steps - 1 - index
                one = past[source, index, 1, at] * stored[source, kept, 0, at]
                two = past[source, index, 0, at] * stored[source, kept, 1, at]
                term = one - two if term is None else term + (one - two)
            total = add_groups(total, term * weight[source], marks[source, at])
    out[...] = jnp.broadcast_to(jnp.sum(total, axis=0, keepdims=True)[None], out.shape)


def group_sums(past, stored, weight, marks, here, devices):
    vmem = pl.BlockSpec(memory_space=pltpu.VMEM)
    return pl.pallas_call(
        sums_kernel,
        out_shape=jax.ShapeDtypeStruct((devices, 1, LANES), jnp.float32),
        in_specs=[IN_PLACE] * 2 + [vmem] * 3,
        out_specs=vmem,
        scratch_shapes=[
            pltpu.VMEM(past.shape, jnp.float32),
            pltpu.VMEM(stored.shape, jnp.float32),
            pltpu.SemaphoreType.DMA((2, past.shape[0])),
        ],
        compiler_params=pltpu.CompilerParams(vmem_limit_bytes=10 * 1024 * 1024),
        name="sums",
    )(kept_out(past), kept_out(stored), weight, marks, here)


def gather_kernel(rank, across, *refs):
    pairs, out = refs[:-1], refs[-1]
    own = across.shape[2]
    for number, pair in enumerate(pairs):
        for side, piece in enumerate((pair[0], across[number])):
            row = pl.multiple_of((rank[0] ^ (2 * number + side)) * own, own)
            out[:, pl.ds(row, own)] = piece


def gather_rows(rank, across, pairs):
    _, _, own, cols = across.shape
    vmem = pl.BlockSpec(memory_space=pltpu.VMEM)
    return pl.pallas_call(
        gather_kernel,
        out_shape=jax.ShapeDtypeStruct((2, 2 * own * len(pairs), cols), jnp.float32),
        in_specs=[SCALARS] + [vmem] * (1 + len(pairs)),
        out_specs=vmem,
        compiler_params=pltpu.CompilerParams(vmem_limit_bytes=8 * 1024 * 1024),
        name="gather",
    )(rank, across, *pairs)


def swap(value, other, count):
    return lax.ppermute(value, "dep", [(i, i ^ other) for i in range(count)])


def on_device(adjoint_in, forward_field, screen, bed_weight, labels):
    steps = forward_field.shape[0]
    sectors = lax.axis_size("az")
    ranges = lax.axis_size("dep")
    position = lax.axis_index("dep")
    rank = position.reshape(1)
    rows_here, cols_here = screen.shape
    own = rows_here // ranges
    halo = 2 * steps
    blocks_here = cols_here // LABEL_BLOCK

    sector, top, bottom = take_edges(adjoint_in, screen, halo)
    ahead = [(i, (i + 1) % sectors) for i in range(sectors)]
    behind = [((i + 1) % sectors, i) for i in range(sectors)]
    above = lax.ppermute(bottom, "az", ahead)
    below = lax.ppermute(top, "az", behind)

    windows = make_windows(sector, above, below, own, halo)
    window = lax.all_to_all(windows, "dep", 0, 0)

    weight = bed_weight.reshape(ranges, 1, cols_here)
    marks_here = lax.dynamic_slice_in_dim(labels, position * blocks_here, blocks_here, 1)
    here = sums_here(rank, adjoint_in, forward_field, weight, marks_here)
    marks = lax.dynamic_slice_in_dim(labels, position * own, own, 0)
    marks = jnp.transpose(marks.reshape(own, ranges, blocks_here), (1, 0, 2))

    stored = forward_field[: steps - 1].reshape(steps - 1, 2, ranges, own, cols_here)
    stored = jnp.transpose(stored, (2, 0, 1, 3, 4))
    window, here, marks, stored = lax.optimization_barrier((window, here, marks, stored))
    stored = lax.all_to_all(stored, "dep", 0, 0)

    past, pairs = run_steps(window, rank, steps, halo)
    pairs = [pairs[0]] + [swap(pairs[number], 2 * number, ranges) for number in range(1, ranges // 2)]
    sums = group_sums(past, stored, weight, marks, here, sectors * ranges)
    _, *ready = lax.optimization_barrier((sums, *pairs))
    across = jnp.stack([pair[1] for pair in ready])
    field = gather_rows(rank, swap(across, 1, ranges), ready)
    sums, field = lax.optimization_barrier((lax.all_to_all(sums, ("az", "dep"), 0, 0), field))
    sums = jnp.sum(sums, axis=(0, 1))[:GROUPS]
    return (field, sums)


def solution(mesh):
    return jax.shard_map(
        on_device,
        mesh=mesh,
        in_specs=(
            P(None, "az", "dep"),
            P(None, None, "az", "dep"),
            P("az", "dep"),
            P(),
            P("az", None),
        ),
        out_specs=(P(None, "az", "dep"), P()),
        check_vma=False,
    )
```
